32 devices in a mesh: section: 2 (over core), expert: 16 (over z, y, x).
Axes of the slice: x: 2, y: 2, z: 4, core: 2. Of those that a mesh axis runs over, the one named last changes fastest.
Arguments:
- tokens: bfloat16 [2, 2048, 2048], P('section', 'expert'), may hold values from -6 to 6
- routes: int32 [2, 2048, 2], P('section', 'expert'), may hold values from 0 to 7, all different within a row; in each aligned block of 128 rows (0 to 127, 128 to 255, ..., all dimensions but the last counted through in order) at most 64 rows name the same one
- probs: bfloat16 [2, 2048, 2], P('section', 'expert'), may hold values from 0.099609375 to 1
- cotangent: bfloat16 [2, 2048, 2048], P('section', 'expert'), may hold values from -6 to 6
- w_gate: bfloat16 [2, 2048, 6144], P('section', None, 'expert'), may hold values from -0.125 to 0.125
- w_up: bfloat16 [2, 2048, 6144], P('section', None, 'expert'), may hold values from -0.125 to 0.125
- w_down: bfloat16 [2, 6144, 2048], P('section', 'expert'), may hold values from -0.21875 to 0.21875
Outputs:
- upstream: bfloat16 [2, 2048, 2048], P('section', 'expert')
- route_grad: bfloat16 [2, 2048, 2], P('section', 'expert')
- grad_gate: bfloat16 [2, 2048, 6144], P('section', None, 'expert')
- grad_up: bfloat16 [2, 2048, 6144], P('section', None, 'expert')
- grad_down: bfloat16 [2, 6144, 2048], P('section', 'expert')
The draws below stay inside these ranges and needn't reach their ends.
Inputs may be any that keep to these rules, and one draw needn't show every extreme that they name: `routes`: each token names 2 different experts. In each aligned block of 128 rows (the tokens of one device) no expert is named by more than 64 rows, and in some blocks one expert is named by exactly 64 rows.
All inputs are finite; a program needn't handle non-finite values.
Results may differ from the reference program's by a relative error of at most 0.008.
Values may be sent and summed in bfloat16 or wider, within the bound.
No kernel may reach another device: no remote copies, remote signals or barrier semaphores. Data moves between devices by JAX's collectives and lax.ppermute only.
A program may use at most 128 MiB of HBM per device.

```python
import math
import jax
import jax.numpy as jnp
import numpy as np
from jax import lax

D = 2048
FF = 768
TOP = 2
TOK_DEV = 128
EXPERTS = 8
CAP = 64
TOKENS = 2048
SECTIONS = 2
N_EXPERT = 16


def level_of(key, shape, split, low, high):
    loudness, own = 1.0, jax.random.fold_in(key, 6)
    for dim, parts in split:
        draws = jnp.exp(jax.random.uniform(jax.random.fold_in(own, dim), (parts,), jnp.float32, low / len(split), high / len(split)))
        loudness = loudness * jnp.repeat(draws, shape[dim] // parts).reshape([-1 if axis == dim else 1 for axis in range(len(shape))])
    return loudness


def routed_block(stream_key, own, number, rows, amount, top, reach, skew):
    ranking = jax.random.permutation(stream_key, amount)
    crowded, ordinary = shares(amount, rows * top, reach, skew, True), shares(amount, rows * top, reach, skew, False)
    places = jnp.arange(amount)

    def named(tallies, rotation):
        used = int((tallies > 0).sum())
        fixed = max(1, used // 4)
        passed = fixed + (places - fixed + rotation * (used - fixed)) % max(1, amount - fixed)
        return jnp.zeros((amount,), jnp.int32).at[ranking[jnp.where(places < fixed, places, passed)]].set(jnp.asarray(tallies, jnp.int32))

    tallies = jnp.where(number % 4 == 0, named(crowded, number // 4), named(ordinary, number - number // 4 - 1))
    mixed = jax.random.permutation(jax.random.fold_in(own, 3), amount)
    donor, receiver = mixed[0:amount // 2 * 2:2], mixed[1:amount // 2 * 2:2]
    slack = jnp.minimum(tallies[donor] - 1, reach - tallies[receiver]) // 2
    slack = jnp.where((donor == ranking[0]) | (receiver == ranking[0]) | (tallies[receiver] == 0), 0, jnp.maximum(slack, 0))
    passed = jax.random.randint(jax.random.fold_in(own, 4), (amount // 2,), 0, 1 << 20) % (slack + 1)
    tallies = tallies.at[donor].add(-passed).at[receiver].add(passed)
    labels = jnp.searchsorted(jnp.cumsum(tallies), jnp.arange(rows * top), side="right").astype(jnp.int32)
    listing = labels.reshape(top, rows).T
    listing = listing[jax.random.permutation(jax.random.fold_in(own, 1), rows)]
    rotation = jax.random.randint(jax.random.fold_in(own, 2), (rows, 1), 0, top)
    return jnp.take_along_axis(listing, (jnp.arange(top)[None, :] + rotation) % top, axis=1)


def shares(number_of, total, reach, skew, full):
    portions = [(1 << 20) // math.isqrt(grade ** skew) + 1 for grade in range(1, number_of + 1)]
    largest = reach if full else min(reach, max(-(-total // number_of), total * portions[0] // sum(portions)))
    least = 1 if total - largest >= number_of - 1 else 0
    counts, rest = [largest] + [least] * (number_of - 1), total - largest - least * (number_of - 1)
    while rest > 0:
        candidates = [i for i in range(1, number_of) if counts[i] < largest] or [i for i in range(1, number_of) if counts[i] < reach]
        mass, left = sum([portions[i] for i in candidates]), rest
        for i in candidates:
            more = min(reach - counts[i], max(1, left * portions[i] // mass), rest)
            counts[i] = counts[i] + more
            rest = rest - more
    return np.array(counts)


def noise(stream_key, dims, width, limit, cuts=(), held_as=jnp.bfloat16):
    level = level_of(stream_key, dims, cuts, -0.22, 0.18) if cuts else 1.0
    drawn = jax.random.normal(stream_key, dims, jnp.float32) * width * level
    return jnp.minimum(jnp.maximum(drawn, -limit), limit).astype(held_as)


def setup_inputs(seed: int = 0) -> dict:
    keys = jax.random.split(jax.random.key(seed), 8)
    tokens = noise(keys[0], (SECTIONS, TOKENS, D), 1.0, 6.0, ((0, 2), (1, 16)))
    routes_keys = jax.random.split(jax.random.fold_in(keys[1], 1), SECTIONS * TOKENS // TOK_DEV)
    routes_turns = jax.random.permutation(jax.random.fold_in(keys[1], 3), SECTIONS * TOKENS // TOK_DEV)
    routes = jax.vmap(lambda own, number: routed_block(jax.random.fold_in(keys[1], 2), own, number, TOK_DEV, EXPERTS, TOP, CAP, 2))(routes_keys, routes_turns).reshape((SECTIONS, TOKENS, TOP))
    probs = jnp.clip(0.099609375 + 0.9003906 * jax.random.uniform(keys[2], (SECTIONS, TOKENS, TOP), jnp.float32) ** level_of(keys[2], (SECTIONS, TOKENS, TOP), ((0, 2), (1, 16)), -0.2, 0.2), 0.099609375, 1.0).astype(jnp.bfloat16)
    cotangent = noise(keys[3], (SECTIONS, TOKENS, D), 1.0, 6.0, ((0, 2), (1, 16)))
    w_gate = noise(keys[4], (SECTIONS, D, EXPERTS * FF), D ** -0.5, 0.125, ((0, 2), (2, 16)))
    w_up = noise(keys[5], (SECTIONS, D, EXPERTS * FF), D ** -0.5, 0.125, ((0, 2), (2, 16)))
    w_down = noise(keys[6], (SECTIONS, EXPERTS * FF, D), FF ** -0.5, 0.21875, ((0, 2), (1, 16)))
    return {"tokens": tokens, "routes": routes, "probs": probs, "cotangent": cotangent, "w_gate": w_gate, "w_up": w_up, "w_down": w_down}


def slot_table(route_rows, experts, capacity):
    flat = route_rows.reshape(-1).astype(jnp.int32)
    count = flat.shape[0]
    onehot = (flat[:, None] == jnp.arange(experts, dtype=jnp.int32)[None, :]).astype(jnp.int32)
    before = jnp.cumsum(onehot, axis=0, dtype=jnp.int32) - onehot
    position = jnp.sum(before * onehot, axis=1, dtype=jnp.int32)
    slot = (flat * capacity + position).astype(jnp.int32)
    owner = jnp.full((experts * capacity,), -1, jnp.int32).at[slot].set(jnp.arange(count, dtype=jnp.int32))
    return slot, owner


def expert_pass(items):
    xin, dyin, pin, wg, wu, wd = items
    pin = pin.astype(jnp.float32)
    gate = jnp.dot(xin, wg, preferred_element_type=jnp.float32)
    up = jnp.dot(xin, wu, preferred_element_type=jnp.float32)
    sig = jax.nn.sigmoid(gate)
    act = gate * sig
    hidden = (act * up).astype(jnp.bfloat16)
    back = lax.dot_general(dyin, wd, (((1,), (1,)), ((), ())), preferred_element_type=jnp.float32)
    route_part = jnp.sum(back * hidden.astype(jnp.float32), axis=1).astype(jnp.bfloat16)
    scaled = pin[:, None] * back
    d_gate = (scaled * up * sig * (1.0 + gate * (1.0 - sig))).astype(jnp.bfloat16)
    d_up = (scaled * act).astype(jnp.bfloat16)
    weighted = (pin[:, None] * hidden.astype(jnp.float32)).astype(jnp.bfloat16)
    g_gate = lax.dot_general(xin, d_gate, (((0,), (0,)), ((), ())), preferred_element_type=jnp.float32).astype(jnp.bfloat16)
    g_up = lax.dot_general(xin, d_up, (((0,), (0,)), ((), ())), preferred_element_type=jnp.float32).astype(jnp.bfloat16)
    g_down = lax.dot_general(weighted, dyin, (((0,), (0,)), ((), ())), preferred_element_type=jnp.float32).astype(jnp.bfloat16)
    part_dx = lax.dot_general(d_gate, wg, (((1,), (1,)), ((), ())), preferred_element_type=jnp.float32)
    part_dx = part_dx + lax.dot_general(d_up, wu, (((1,), (1,)), ((), ())), preferred_element_type=jnp.float32)
    return g_gate, g_up, g_down, part_dx.astype(jnp.bfloat16), route_part


def reference(tokens, routes, probs, cotangent, w_gate, w_up, w_down):
    def pack_source(rows_x, rows_r, rows_p, rows_dy):
        slot, owner = slot_table(rows_r, EXPERTS, CAP)
        valid = owner >= 0
        entry = jnp.maximum(owner, 0)
        token_of = entry // TOP
        send_x = jnp.where(valid[:, None], rows_x[token_of], jnp.zeros((), jnp.bfloat16)).astype(jnp.bfloat16)
        send_dy = jnp.where(valid[:, None], rows_dy[token_of], jnp.zeros((), jnp.bfloat16)).astype(jnp.bfloat16)
        send_p = jnp.where(valid, rows_p.reshape(-1)[entry], jnp.zeros((), jnp.bfloat16)).astype(jnp.bfloat16)
        return slot, send_x.reshape(EXPERTS, CAP, D), send_dy.reshape(EXPERTS, CAP, D), send_p.reshape(EXPERTS, CAP)

    def unpack(table, route_table, slot):
        rows = table[slot].astype(jnp.float32).reshape(TOK_DEV, TOP, D).sum(axis=1).astype(jnp.bfloat16)
        return rows, route_table[slot].reshape(TOK_DEV, TOP)

    def one_section(items):
        layer_x, layer_r, layer_p, layer_dy, wg, wu, wd = items
        slots, box_x, box_dy, box_p = jax.vmap(pack_source)(
            layer_x.reshape(N_EXPERT, TOK_DEV, D), layer_r.reshape(N_EXPERT, TOK_DEV, TOP),
            layer_p.reshape(N_EXPERT, TOK_DEV, TOP), layer_dy.reshape(N_EXPERT, TOK_DEV, D))
        box_x = box_x.transpose(1, 0, 2, 3).reshape(EXPERTS, N_EXPERT * CAP, D)
        box_dy = box_dy.transpose(1, 0, 2, 3).reshape(EXPERTS, N_EXPERT * CAP, D)
        box_p = box_p.transpose(1, 0, 2).reshape(EXPERTS, N_EXPERT * CAP)
        wg_each = wg.reshape(D, EXPERTS, FF).transpose(1, 0, 2)
        wu_each = wu.reshape(D, EXPERTS, FF).transpose(1, 0, 2)
        wd_each = wd.reshape(EXPERTS, FF, D)
        g_gate, g_up, g_down, part_dx, route_part = lax.map(expert_pass, (box_x, box_dy, box_p, wg_each, wu_each, wd_each))
        part_dx = part_dx.reshape(EXPERTS, N_EXPERT, CAP, D).transpose(1, 0, 2, 3).reshape(N_EXPERT, EXPERTS * CAP, D)
        route_part = route_part.reshape(EXPERTS, N_EXPERT, CAP).transpose(1, 0, 2).reshape(N_EXPERT, EXPERTS * CAP)
        layer_dx, layer_route = jax.vmap(unpack)(part_dx, route_part, slots)
        return (layer_dx.reshape(TOKENS, D), layer_route.reshape(TOKENS, TOP),
                g_gate.transpose(1, 0, 2).reshape(D, EXPERTS * FF),
                g_up.transpose(1, 0, 2).reshape(D, EXPERTS * FF),
                g_down.reshape(EXPERTS * FF, D))

    dx, route_grad, grad_gate, grad_up, grad_down = lax.map(one_section, (tokens, routes, probs, cotangent, w_gate, w_up, w_down))
    upstream = jnp.concatenate([dx[1:], jnp.zeros_like(dx[:1])], axis=0)
    return (upstream, route_grad, grad_gate, grad_up, grad_down)
```

```python
import jax
import jax.numpy as jnp
from jax import lax
from jax.sharding import PartitionSpec as P

AXES = ("section", "expert")
GROUP = 2


def shifted(value, mask, first=0):
    sections, units = lax.axis_size("section"), lax.axis_size("expert")
    pairs = [
        (s * units + i, s * units + (i ^ mask)) for s in range(first, sections) for i in range(units)
    ]
    return lax.ppermute(value, AXES, pairs)


def dot(a, b, ca, cb):
    return lax.dot_general(a, b, (((ca,), (cb,)), ((), ())), preferred_element_type=jnp.float32)


def body(tokens, routes, probs, cotangent, w_gate, w_up, w_down):
    units = lax.axis_size("expert")
    experts = units // 2
    rows, width = tokens.shape[1], tokens.shape[2]
    top = routes.shape[2]
    cap = 2 * rows * top // experts
    me = lax.axis_index("expert")
    home = me // 2
    half = jnp.bfloat16
    wg, wu, wd = w_gate[0], w_up[0], w_down[0]

    near_expert = routes[0] ^ home
    names = near_expert[:, :, None] == jnp.arange(experts, dtype=jnp.int32)
    named = jnp.sum(names.astype(jnp.float32), axis=1)
    weight = jnp.sum(names.astype(jnp.float32) * probs[0].astype(jnp.float32)[:, :, None], axis=1)
    before = (
        lax.broadcasted_iota(jnp.int32, (rows, rows), 1)
        < lax.broadcasted_iota(jnp.int32, (rows, rows), 0)
    )
    place = dot(before.astype(half), named.astype(half), 1, 0)
    place = jnp.where(named > 0, place, -1.0).T
    pick = place[:, None, :] == jnp.arange(cap, dtype=jnp.float32)[None, :, None]
    pick_x = pick.astype(half)
    pick_g = jnp.where(pick, weight.T[:, None, :], 0.0).astype(half)
    send_x = dot(pick_x.reshape(experts * cap, rows), tokens[0], 1, 0).astype(half)
    send_g = dot(pick_g.reshape(experts * cap, rows), cotangent[0], 1, 0).astype(half)
    box = jnp.stack(
        [send_x.reshape(experts, cap, width), send_g.reshape(experts, cap, width)], axis=1
    )

    near = [box[0]] + [shifted(box[d], 2 * d) for d in range(1, experts)]
    far = [shifted(block, 1) for block in near]

    das, dbs, hs, near_rg, far_rg = [], [], [], [], []
    got = []
    for c in range(0, experts, GROUP):
        blocks = near[c : c + GROUP] + far[c : c + GROUP]
        x = jnp.concatenate([b[0] for b in blocks], axis=0)
        g = jnp.concatenate([b[1] for b in blocks], axis=0)
        a = dot(x, wg, 1, 0)
        b = dot(x, wu, 1, 0)
        q = dot(g, wd, 1, 1)
        sig = jax.nn.sigmoid(a)
        act = a * sig
        h = (act * b).astype(half)
        rg = jnp.sum(q * h.astype(jnp.float32), axis=1).reshape(2, GROUP, cap)
        da = (q * b * sig * (1.0 + a * (1.0 - sig))).astype(half)
        db = (q * act).astype(half)
        das.append(da)
        dbs.append(db)
        hs.append(h)
        near_rg.append(rg[0])
        far_rg.append(rg[1])
        part = dot(da, wg, 1, 1) + dot(db, wu, 1, 1)
        part = part.reshape(2, GROUP, cap, width)
        partner = shifted(part[1].astype(half), 1, 1)
        total = (part[0] + partner).astype(half)
        for i in range(GROUP):
            got.append(total[i] if c + i == 0 else shifted(total[i], 2 * (c + i), 1))

    ordered = [
        b for c in range(0, experts, GROUP) for b in near[c : c + GROUP] + far[c : c + GROUP]
    ]
    x_all = jnp.concatenate([b[0] for b in ordered], axis=0)
    g_all = jnp.concatenate([b[1] for b in ordered], axis=0)
    da_all, db_all, h_all = (jnp.concatenate(v, axis=0) for v in (das, dbs, hs))
    g_gate = dot(x_all, da_all, 0, 0).astype(half)
    g_up = dot(x_all, db_all, 0, 0).astype(half)
    g_down = dot(h_all, g_all, 0, 0).astype(half)

    rg_all = jnp.stack(
        [jnp.concatenate(near_rg, axis=0), jnp.concatenate(far_rg, axis=0)], axis=1
    ).reshape(units, cap)
    here = jnp.arange(units, dtype=jnp.int32)
    rg_sent = rg_all[here ^ me]
    rg_back = lax.all_to_all(rg_sent, "expert", split_axis=0, concat_axis=0, tiled=True)
    rg_slot = rg_back[here ^ me].reshape(experts, 2, cap).sum(axis=1)
    rg_named = jnp.sum(jnp.where(pick, rg_slot[:, :, None], 0.0), axis=1).T
    rg_token = jnp.sum(jnp.where(names, rg_named[:, None, :], 0.0), axis=2)
    route_grad = (rg_token / probs[0].astype(jnp.float32)).astype(half)

    back = jnp.concatenate(got, axis=0)
    layer_dx = dot(pick_x.reshape(experts * cap, rows), back, 0, 0).astype(half)
    sections = lax.axis_size("section")
    upstream = lax.ppermute(layer_dx, "section", [(s, s - 1) for s in range(1, sections)])
    return (upstream[None], route_grad[None], g_gate[None], g_up[None], g_down[None])


def solution(mesh):
    rows, columns = P("section", "expert", None), P("section", None, "expert")
    in_specs = (rows, rows, rows, rows, columns, columns, rows)
    out_specs = (rows, rows, columns, columns, rows)
    return jax.shard_map(body, mesh=mesh, in_specs=in_specs, out_specs=out_specs, check_vma=False)
```

```python
import jax
import jax.numpy as jnp
from jax import lax
from jax.sharding import PartitionSpec as P


AXES = ("section", "expert")


def offsets_of(experts):
    return sorted(range(experts), key=lambda d: (d.bit_count(), d))


def groups_of(experts):
    order = offsets_of(experts)
    pairs = [order[i : i + 2] for i in range(0, experts - 2, 2)]
    return pairs + [[d] for d in order[experts - 2 :]]


def shifted(value, mask, first=0):
    sections, units = lax.axis_size("section"), lax.axis_size("expert")
    pairs = [
        (s * units + i, s * units + (i ^ mask)) for s in range(first, sections) for i in range(units)
    ]
    return lax.ppermute(value, AXES, pairs)


def dot(a, b, ca, cb):
    return lax.dot_general(a, b, (((ca,), (cb,)), ((), ())), preferred_element_type=jnp.float32)


def body(tokens, routes, probs, cotangent, w_gate, w_up, w_down):
    units = lax.axis_size("expert")
    experts = units // 2
    rows, width = tokens.shape[1], tokens.shape[2]
    top = routes.shape[2]
    cap = 2 * rows * top // experts
    me = lax.axis_index("expert")
    home = me // 2
    half = jnp.bfloat16
    wg, wu, wd = w_gate[0], w_up[0], w_down[0]

    near_expert = routes[0] ^ home
    names = near_expert[:, :, None] == jnp.arange(experts, dtype=jnp.int32)
    named = jnp.sum(names.astype(jnp.float32), axis=1)
    weight = jnp.sum(names.astype(jnp.float32) * probs[0].astype(jnp.float32)[:, :, None], axis=1)
    before = (
        lax.broadcasted_iota(jnp.int32, (rows, rows), 1)
        < lax.broadcasted_iota(jnp.int32, (rows, rows), 0)
    )
    place = dot(before.astype(half), named.astype(half), 1, 0)
    place = jnp.where(named > 0, place, -1.0).T
    pick = place[:, None, :] == jnp.arange(cap, dtype=jnp.float32)[None, :, None]
    pick_x = pick.astype(half)
    pick_g = jnp.where(pick, weight.T[:, None, :], 0.0).astype(half)
    send_x = dot(pick_x.reshape(experts * cap, rows), tokens[0], 1, 0).astype(half)
    send_g = dot(pick_g.reshape(experts * cap, rows), cotangent[0], 1, 0).astype(half)
    box = jnp.stack(
        [send_x.reshape(experts, cap, width), send_g.reshape(experts, cap, width)], axis=1
    )

    order = offsets_of(experts)
    near = {d: shifted(box[d], 2 * d) for d in order[1:]}
    near[0] = box[0]
    far = {d: shifted(near[d], 1) for d in order}

    das, dbs, hs, near_rg, far_rg, got = [], [], [], {}, {}, {}
    for group in groups_of(experts):
        size = len(group)
        blocks = [near[d] for d in group] + [far[d] for d in group]
        x = jnp.concatenate([b[0] for b in blocks], axis=0)
        g = jnp.concatenate([b[1] for b in blocks], axis=0)
        a = dot(x, wg, 1, 0)
        b = dot(x, wu, 1, 0)
        q = dot(g, wd, 1, 1)
        sig = jax.nn.sigmoid(a)
        act = a * sig
        h = (act * b).astype(half)
        rg = jnp.sum(q * h.astype(jnp.float32), axis=1).reshape(2, size, cap)
        da = (q * b * sig * (1.0 + a * (1.0 - sig))).astype(half)
        db = (q * act).astype(half)
        das.append(da)
        dbs.append(db)
        hs.append(h)
        part = dot(da, wg, 1, 1) + dot(db, wu, 1, 1)
        part = part.reshape(2, size, cap, width)
        partner = shifted(part[1].astype(half), 1, 1)
        total = (part[0] + partner).astype(half)
        for i, d in enumerate(group):
            near_rg[d], far_rg[d] = rg[0, i], rg[1, i]
            got[d] = total[i] if d == 0 else shifted(total[i], 2 * d, 1)

    ordered = [
        source[d] for group in groups_of(experts) for source in (near, far) for d in group
    ]
    x_all = jnp.concatenate([b[0] for b in ordered], axis=0)
    g_all = jnp.concatenate([b[1] for b in ordered], axis=0)
    da_all, db_all, h_all = (jnp.concatenate(v, axis=0) for v in (das, dbs, hs))
    g_gate = dot(x_all, da_all, 0, 0).astype(half)
    g_up = dot(x_all, db_all, 0, 0).astype(half)
    g_down = dot(h_all, g_all, 0, 0).astype(half)

    rg_slot = jnp.stack([near_rg[d] for d in range(experts)])
    rg_far = jnp.stack([far_rg[d] for d in range(experts)])
    rg_slot = rg_slot + shifted(rg_far, 1)
    for bit in range(experts.bit_length() - 1):
        high = [d for d in range(experts) if d >> bit & 1]
        moved = shifted(jnp.stack([rg_slot[d] for d in high]), 2 << bit)
        rg_slot = jnp.stack(
            [moved[high.index(d)] if d in high else rg_slot[d] for d in range(experts)]
        )
    rg_named = jnp.sum(jnp.where(pick, rg_slot[:, :, None], 0.0), axis=1).T
    rg_token = jnp.sum(jnp.where(names, rg_named[:, None, :], 0.0), axis=2)
    route_grad = (rg_token / probs[0].astype(jnp.float32)).astype(half)

    back = jnp.concatenate([got[d] for d in range(experts)], axis=0)
    layer_dx = dot(pick_x.reshape(experts * cap, rows), back, 0, 0).astype(half)
    sections = lax.axis_size("section")
    upstream = lax.ppermute(layer_dx, "section", [(s, s - 1) for s in range(1, sections)])
    return (upstream[None], route_grad[None], g_gate[None], g_up[None], g_down[None])


def solution(mesh):
    rows, columns = P("section", "expert", None), P("section", None, "expert")
    in_specs = (rows, rows, rows, rows, columns, columns, rows)
    out_specs = (rows, rows, columns, columns, rows)

    return jax.shard_map(body, mesh=mesh, in_specs=in_specs, out_specs=out_specs, check_vma=False)
```

```python
import functools

import jax
import jax.numpy as jnp
from jax import lax
from jax.experimental import pallas as pl
from jax.experimental.pallas import tpu as pltpu
from jax.sharding import PartitionSpec as P


AXES = ("section", "expert")
HALF, FULL = jnp.bfloat16, jnp.float32
LINE = 4
VMEM = pl.BlockSpec(memory_space=pltpu.VMEM)
SMEM = pl.BlockSpec(memory_space=pltpu.SMEM)
ANY = pl.BlockSpec(memory_space=pl.ANY)


def moved(value, target, first=0, down=0):
    sections, units = lax.axis_size("section"), lax.axis_size("expert")
    pairs = [
        (s * units + i, (s - down) * units + target(i))
        for s in range(first, sections)
        for i in range(units)
        if target(i) is not None
    ]
    return lax.ppermute(value, AXES, pairs)


def shifted(value, mask, first=0, down=0):
    return moved(value, lambda i: i ^ mask, first, down)


def groups_of(experts):
    ring = experts // LINE
    size = min(2, ring)
    head = [list(range(i, i + size)) for i in range(0, experts - size, size)]
    return head + [[o] for o in range(experts - size, experts)]


def dot(a, b, ca, cb):
    return lax.dot_general(a, b, (((ca,), (cb,)), ((), ())), preferred_element_type=FULL)


def picks(code, home, offsets, cap):
    top, rows = code.shape[0] // 2, code.shape[1]
    near = [code[k : k + 1].astype(jnp.int32) ^ home for k in range(top)]
    hits = [[n == o for n in near] for o in offsets]
    named = jnp.concatenate(
        [functools.reduce(jnp.logical_or, h).astype(FULL) for h in hits], axis=0
    )
    weight = [
        functools.reduce(
            jnp.add, [jnp.where(h[k], code[top + k : top + k + 1], 0.0) for k in range(top)]
        )
        for h in hits
    ]
    earlier = (
        lax.broadcasted_iota(jnp.int32, (rows, rows), 0)
        < lax.broadcasted_iota(jnp.int32, (rows, rows), 1)
    )
    place = dot(named.astype(HALF), earlier.astype(FULL).astype(HALF), 1, 0)
    place = jnp.where(named > 0, place, -1.0)
    slot = lax.broadcasted_iota(jnp.int32, (cap, rows), 0).astype(FULL)
    return [slot == place[i : i + 1] for i in range(len(offsets))], weight


def select_kernel(sources, ring, cap, where_ref, code_ref, *refs):
    source, out, (held, sem) = refs[:sources], refs[sources : sources + ring], refs[-2:]
    for i in range(sources):

        @pl.when(where_ref[1] == i)
        def _():
            pltpu.make_async_copy(source[i], held, sem).start()

    pick, weight = picks(code_ref[...], where_ref[0], range(ring), cap)
    pltpu.make_async_copy(source[0], held, sem).wait()
    for d in range(ring):
        rows_x = jnp.where(pick[d], 1.0, 0.0).astype(HALF)
        rows_g = jnp.where(pick[d], weight[d], 0.0).astype(HALF)
        out[d][0] = dot(rows_x, held[0], 1, 0).astype(HALF)
        out[d][1] = dot(rows_g, held[1], 1, 0).astype(HALF)


def select(where, code, sources, ring, cap):
    two, rows, width = sources[0].shape
    return pl.pallas_call(
        functools.partial(select_kernel, len(sources), ring, cap),
        out_shape=[jax.ShapeDtypeStruct((two, cap, width), HALF)] * ring,
        in_specs=[SMEM, VMEM] + [ANY] * len(sources),
        out_specs=[VMEM] * ring,
        scratch_shapes=[pltpu.VMEM((two, rows, width), HALF), pltpu.SemaphoreType.DMA],
        name="select",
    )(where, code, *sources)


def phase_kernel(size, *refs):
    near, far, (wg, wu, wd) = refs[:size], refs[size : 2 * size], refs[2 * size : 2 * size + 3]
    da_ref, db_ref, h_ref, rg_ref, *parts = refs[2 * size + 3 :]
    cap = near[0].shape[1]
    x = jnp.concatenate([r[0] for r in near + far], axis=0)
    g = jnp.concatenate([r[1] for r in near + far], axis=0)
    a = dot(x, wg[...], 1, 0)
    b = dot(x, wu[...], 1, 0)
    q = dot(g, wd[...], 1, 1)
    sig = jax.nn.sigmoid(a)
    act = a * sig
    h = (act * b).astype(HALF)
    rg_ref[...] = jnp.sum(q * h.astype(FULL), axis=1, keepdims=True)
    da = (q * b * sig * (1.0 + a * (1.0 - sig))).astype(HALF)
    db = (q * act).astype(HALF)
    h_ref[...], da_ref[...], db_ref[...] = h, da, db
    part = (dot(da, wg[...], 1, 1) + dot(db, wu[...], 1, 1)).astype(HALF)
    for i in range(size):
        for side in range(2):
            start = (side * size + i) * cap
            parts[i][side] = part[start : start + cap]


def phase(near, far, wg, wu, wd):
    size = len(near)
    _, cap, width = near[0].shape
    rows, hidden = 2 * size * cap, wg.shape[1]
    flat = jax.ShapeDtypeStruct((rows, hidden), HALF)
    da, db, h, rg, *parts = pl.pallas_call(
        functools.partial(phase_kernel, size),
        out_shape=[flat, flat, flat, jax.ShapeDtypeStruct((rows, 1), FULL)]
        + [jax.ShapeDtypeStruct((2, cap, width), HALF)] * size,
        in_specs=[VMEM] * (2 * size + 3),
        out_specs=[VMEM] * (4 + size),
        name="phase",
    )(*near, *far, wg, wu, wd)
    return da, db, h, rg.reshape(2, size, cap), parts


def grads_kernel(count, chunks, *refs):
    blocks = refs[:count]
    das, dbs, hs = (refs[count + i * chunks : count + (i + 1) * chunks] for i in range(3))
    gate_ref, up_ref, down_ref = refs[-3:]
    x = jnp.concatenate([r[0] for r in blocks], axis=0)
    g = jnp.concatenate([r[1] for r in blocks], axis=0)
    da, db, h = (jnp.concatenate([r[...] for r in refs_], axis=0) for refs_ in (das, dbs, hs))
    gate_ref[...] = dot(x, da, 0, 0).astype(HALF)
    up_ref[...] = dot(x, db, 0, 0).astype(HALF)
    down_ref[...] = dot(h, g, 0, 0).astype(HALF)


def grads(blocks, das, dbs, hs, hidden, tile=512):
    _, cap, width = blocks[0].shape
    flat = list(das) + list(dbs) + list(hs)
    return pl.pallas_call(
        functools.partial(grads_kernel, len(blocks), len(das)),
        grid=(width // tile,),
        out_shape=[
            jax.ShapeDtypeStruct((width, hidden), HALF),
            jax.ShapeDtypeStruct((width, hidden), HALF),
            jax.ShapeDtypeStruct((hidden, width), HALF),
        ],
        in_specs=[pl.BlockSpec((2, cap, tile), lambda i: (0, 0, i))] * len(blocks)
        + [pl.BlockSpec(v.shape, lambda i: (0, 0)) for v in flat],
        out_specs=[
            pl.BlockSpec((tile, hidden), lambda i: (i, 0)),
            pl.BlockSpec((tile, hidden), lambda i: (i, 0)),
            pl.BlockSpec((hidden, tile), lambda i: (0, i)),
        ],
        name="grads",
    )(*blocks, *flat)


def combine_kernel(experts, cap, where_ref, mine_ref, other_ref, *refs):
    got, (near_ref, far_ref) = refs[:experts], refs[experts:]
    for side, code_ref, out in ((0, mine_ref, near_ref), (1, other_ref, far_ref)):
        pick, _ = picks(code_ref[...], where_ref[0], range(experts), cap)
        rows = jnp.concatenate([jnp.where(p, 1.0, 0.0).astype(HALF) for p in pick], axis=0)
        back = jnp.concatenate([r[side] for r in got], axis=0)
        out[...] = dot(rows, back, 0, 0).astype(HALF)


def combine(where, mine, other, got, tile=1024):
    _, cap, width = got[0].shape
    rows = mine.shape[1]
    code = pl.BlockSpec(mine.shape, lambda i: (0, 0))
    return pl.pallas_call(
        functools.partial(combine_kernel, len(got), cap),
        grid=(width // tile,),
        out_shape=[jax.ShapeDtypeStruct((rows, width), HALF)] * 2,
        in_specs=[SMEM, code, code]
        + [pl.BlockSpec((2, cap, tile), lambda i: (0, 0, i))] * len(got),
        out_specs=[pl.BlockSpec((rows, tile), lambda i: (0, i))] * 2,
        name="combine",
    )(where, mine, other, *got)


def body(tokens, routes, probs, cotangent, w_gate, w_up, w_down):
    units = lax.axis_size("expert")
    experts = units // 2
    ring = experts // LINE
    rows, top = routes.shape[1:]
    cap = 2 * rows * top // experts
    home = lax.axis_index("expert") // 2
    line = home // ring
    wg, wu, wd = w_gate[0], w_up[0], w_down[0]
    hidden = wg.shape[1]
    inner = ((line == 1) | (line == 2)).astype(jnp.int32)
    where_one = jnp.stack([home, jnp.zeros_like(home)]).astype(jnp.int32)
    where_two = jnp.stack([home, 1 - inner]).astype(jnp.int32)

    def along(value, hops):
        step = 2 * ring

        def target(i):
            return hops[i // step] * step + i % step if i // step in hops else None

        return moved(value, target)

    own = jnp.stack([tokens[0], cotangent[0]])
    code = jnp.concatenate([routes[0].astype(FULL).T, probs[0].astype(FULL).T], axis=0)
    side1 = along(own, {0: 1, 1: 0, 2: 3, 3: 2})
    side2 = along(own, {1: 2, 2: 1})
    side3 = along(side1, {1: 2, 2: 1})
    side4 = along(side2, {1: 0, 2: 3})
    side5 = along(side3, {1: 0, 2: 3})
    codes = [code] + [shifted(code, 2 * ring * j) for j in range(1, LINE)]
    mirror = shifted(code, 1)

    sources = [(where_one, [own]), (where_one, [side1])]
    sources += [(where_two, [side3, side4]), (where_two, [side2, side5])]
    near, far = {}, {}
    for j, (where, source) in enumerate(sources):
        for d, block in enumerate(select(where, codes[j], source, ring, cap)):
            o = j * ring + d
            near[o] = block if d == 0 else shifted(block, 2 * d)
            far[o] = shifted(near[o], 1)

    das, dbs, hs, blocks, near_rg, far_rg, got = [], [], [], [], {}, {}, {}
    for group in groups_of(experts):
        near_group, far_group = [near[o] for o in group], [far[o] for o in group]
        da, db, h, rg, parts = phase(near_group, far_group, wg, wu, wd)
        das, dbs, hs = das + [da], dbs + [db], hs + [h]
        blocks += near_group + far_group
        for i, o in enumerate(group):
            near_rg[o], far_rg[o] = rg[0, i], rg[1, i]
            got[o] = parts[i] if o == 0 else shifted(parts[i], 2 * o, 1)

    g_gate, g_up, g_down = grads(blocks, das, dbs, hs, hidden)

    slots = jnp.stack([near_rg[o] for o in range(experts)])
    slots += shifted(jnp.stack([far_rg[o] for o in range(experts)]), 1)
    for bit in range(experts.bit_length() - 1):
        high = [o for o in range(experts) if o >> bit & 1]
        taken = shifted(jnp.stack([slots[o] for o in high]), 2 << bit)
        slots = jnp.stack(
            [taken[high.index(o)] if o in high else slots[o] for o in range(experts)]
        )
    near_expert = routes[0] ^ home
    names = near_expert[:, :, None] == jnp.arange(experts, dtype=jnp.int32)
    named = jnp.sum(names.astype(FULL), axis=1)
    earlier = (
        lax.broadcasted_iota(jnp.int32, (rows, rows), 1)
        < lax.broadcasted_iota(jnp.int32, (rows, rows), 0)
    )
    place = dot(earlier.astype(HALF), named.astype(HALF), 1, 0)
    place = jnp.where(named > 0, place, -1.0).T
    pick = place[:, None, :] == jnp.arange(cap, dtype=FULL)[None, :, None]
    rg_named = jnp.sum(jnp.where(pick, slots[:, :, None], 0.0), axis=1).T
    rg_token = jnp.sum(jnp.where(names, rg_named[:, None, :], 0.0), axis=2)
    route_grad = (rg_token / probs[0].astype(FULL)).astype(HALF)

    dx_near, dx_far = combine(where_one, code, mirror, [got[o] for o in range(experts)])
    below = shifted(dx_near, 0, 1, 1)
    across = shifted(dx_far, 1, 1, 1)
    upstream = (below.astype(FULL) + across.astype(FULL)).astype(HALF)
    return (upstream[None], route_grad[None], g_gate[None], g_up[None], g_down[None])


def solution(mesh):
    rows, columns = P("section", "expert", None), P("section", None, "expert")
    in_specs = (rows, rows, rows, rows, columns, columns, rows)
    out_specs = (rows, rows, columns, columns, rows)

    return jax.shard_map(body, mesh=mesh, in_specs=in_specs, out_specs=out_specs, check_vma=False)
```

```python
import functools

import jax
import jax.numpy as jnp
from jax import lax
from jax.experimental import pallas as pl
from jax.experimental.pallas import tpu as pltpu
from jax.sharding import PartitionSpec as P


AXES = ("section", "expert")
HALF, FULL = jnp.bfloat16, jnp.float32
LINE = 4
VMEM = pl.BlockSpec(memory_space=pltpu.VMEM)
ANY = pl.BlockSpec(memory_space=pl.ANY)
ROOM = pltpu.CompilerParams(vmem_limit_bytes=28 << 20)


def moved(value, target, first=0, down=0):
    sections, units = lax.axis_size("section"), lax.axis_size("expert")
    pairs = [
        (s * units + i, (s - down) * units + target(i))
        for s in range(first, sections)
        for i in range(units)
        if target(i) is not None
    ]
    return lax.ppermute(value, AXES, pairs)


def shifted(value, mask, first=0, down=0):
    return moved(value, lambda i: i ^ mask, first, down)


def groups_of(experts):
    ring = experts // LINE
    head = [list(range(2 * ring)), list(range(2 * ring, experts - 2))]
    return [group for group in head if group] + [[experts - 2], [experts - 1]]


def kept(shape, kind):
    return pltpu.VMEM(shape, kind)


def position(experts):
    home = lax.axis_index("expert") // 2
    line = home // (experts // LINE)
    return home, jnp.logical_or(line == 1, line == 2)


def dot(a, b, ca, cb):
    return lax.dot_general(a, b, (((ca,), (cb,)), ((), ())), preferred_element_type=FULL)


def picks(code, home, offsets, cap):
    top, rows = code.shape[0] // 2, code.shape[1]
    near = [code[k : k + 1].astype(jnp.int32) ^ home for k in range(top)]
    hits = [[n == o for n in near] for o in offsets]
    named = jnp.concatenate(
        [functools.reduce(jnp.logical_or, h).astype(FULL) for h in hits], axis=0
    )
    weight = [
        functools.reduce(
            jnp.add, [jnp.where(h[k], code[top + k : top + k + 1], 0.0) for k in range(top)]
        )
        for h in hits
    ]
    earlier = (
        lax.broadcasted_iota(jnp.int32, (rows, rows), 0)
        < lax.broadcasted_iota(jnp.int32, (rows, rows), 1)
    )
    place = dot(named.astype(HALF), earlier.astype(FULL).astype(HALF), 1, 0)
    place = jnp.where(named > 0, place, -1.0)
    slot = lax.broadcasted_iota(jnp.int32, (cap, rows), 0).astype(FULL)
    return [slot == place[i : i + 1] for i in range(len(offsets))], weight


def load_kernel(*refs):
    count, sem = len(refs) // 2, refs[-1]
    copies = [pltpu.make_async_copy(refs[i], refs[count + i], sem.at[i]) for i in range(count)]
    for copy in copies:
        copy.start()
    for copy in copies:
        copy.wait()


def load(*arrays):
    return pl.pallas_call(
        load_kernel,
        out_shape=[kept(v.shape, v.dtype) for v in arrays],
        in_specs=[ANY] * len(arrays),
        out_specs=[VMEM] * len(arrays),
        scratch_shapes=[pltpu.SemaphoreType.DMA((len(arrays),))],
        name="load",
        compiler_params=ROOM,
    )(*arrays)


def select_kernel(sources, experts, cap, code_ref, *refs):
    ring = experts // LINE
    home, inner = position(experts)
    from_x, from_g = refs[:sources], refs[sources : 2 * sources]
    out, (x_held, g_held, sem) = refs[2 * sources : 2 * sources + ring], refs[-3:]

    def fetch(i):
        pltpu.make_async_copy(from_x[i], x_held, sem.at[0]).start()
        pltpu.make_async_copy(from_g[i], g_held, sem.at[1]).start()

    if sources == 1:
        fetch(0)
    else:
        pl.when(inner)(lambda: fetch(0))
        pl.when(jnp.logical_not(inner))(lambda: fetch(1))
    pick, weight = picks(code_ref[...], home, range(ring), cap)
    rows_x = jnp.concatenate([jnp.where(p, 1.0, 0.0) for p in pick], axis=0).astype(HALF)
    rows_g = jnp.concatenate([jnp.where(p, w, 0.0) for p, w in zip(pick, weight)], axis=0)
    pltpu.make_async_copy(from_x[0], x_held, sem.at[0]).wait()
    x = dot(rows_x, x_held[...], 1, 0).astype(HALF)
    for d in range(ring):
        out[d][0] = x[d * cap : (d + 1) * cap]
    pltpu.make_async_copy(from_g[0], g_held, sem.at[1]).wait()
    g = dot(rows_g.astype(HALF), g_held[...], 1, 0).astype(HALF)
    for d in range(ring):
        out[d][1] = g[d * cap : (d + 1) * cap]


def select(code, from_x, from_g, experts, cap):
    rows, width = from_x[0].shape
    ring = experts // LINE
    return pl.pallas_call(
        functools.partial(select_kernel, len(from_x), experts, cap),
        out_shape=[kept((2, cap, width), HALF)] * ring,
        in_specs=[VMEM] + [ANY] * (2 * len(from_x)),
        out_specs=[VMEM] * ring,
        scratch_shapes=[pltpu.VMEM((rows, width), HALF)] * 2 + [pltpu.SemaphoreType.DMA((2,))],
        name="select",
        compiler_params=ROOM,
    )(code, *from_x, *from_g)


def phase_kernel(size, reduced, *refs):
    near, far, (wg, wu, wd) = refs[:size], refs[size : 2 * size], refs[2 * size : 2 * size + 3]
    x_ref, g_ref, da_ref, db_ref, h_ref, rg_ref, *parts, sem = refs[2 * size + 3 :]
    cap = near[0].shape[1]
    for which, held in enumerate((x_ref, g_ref)):
        for i, ref in enumerate(near + far):
            rows = held.at[pl.ds(i * cap, cap)]
            pltpu.make_async_copy(ref.at[which], rows, sem.at[which]).start()
    pltpu.make_async_copy(x_ref, x_ref, sem.at[0]).wait()
    a = dot(x_ref[...], wg[...], 1, 0)
    b = dot(x_ref[...], wu[...], 1, 0)
    pltpu.make_async_copy(g_ref, g_ref, sem.at[1]).wait()
    q = dot(g_ref[...], wd[...], 1, 1)
    sig = jax.nn.sigmoid(a)
    act = a * sig
    h = (act * b).astype(HALF)
    da = (q * b * sig * (1.0 + a * (1.0 - sig))).astype(HALF)
    db = (q * act).astype(HALF)
    h_ref[...], da_ref[...], db_ref[...] = h, da, db
    rg_ref[...] = jnp.sum((q * h.astype(FULL)).reshape(2 * size, cap, -1), axis=2)
    part = dot(da, wg[...], 1, 1) + dot(db, wu[...], 1, 1)
    for i in range(size):
        for side in range(2):
            start = (side * size + i) * cap
            piece = part[start : start + cap]
            if reduced:
                parts[2 * i + side][...] = piece if side == 0 else piece.astype(HALF)
            else:
                parts[i][side] = piece.astype(HALF)


def phase(near, far, wg, wu, wd, reduced):
    size = len(near)
    _, cap, width = near[0].shape
    rows, hidden = 2 * size * cap, wg.shape[1]
    if reduced:
        parts = [kept((cap, width), t) for t in (FULL, HALF)] * size
    else:
        parts = [kept((2, cap, width), HALF)] * size
    out = pl.pallas_call(
        functools.partial(phase_kernel, size, reduced),
        out_shape=[kept((rows, width), HALF)] * 2
        + [kept((rows, hidden), HALF)] * 3
        + [kept((2 * size, cap), FULL)]
        + parts,
        in_specs=[ANY] * (2 * size) + [VMEM] * 3,
        out_specs=[VMEM] * (6 + len(parts)),
        scratch_shapes=[pltpu.SemaphoreType.DMA((2,))],
        name="phase",
        compiler_params=ROOM,
    )(*near, *far, wg, wu, wd)
    return out[:5], out[5], out[6:]


def grads_kernel(count, begun, last, tile, *refs):
    xs, gs, das, dbs, hs = (refs[i * count : (i + 1) * count] for i in range(5))
    olds, outs = refs[5 * count : -3], refs[-3:]
    start = pl.multiple_of(pl.program_id(0) * tile, tile)
    cols = pl.ds(start, tile)
    x = jnp.concatenate([r[:, cols] for r in xs], axis=0)
    g = jnp.concatenate([r[:, cols] for r in gs], axis=0)
    da, db, h = (jnp.concatenate([r[...] for r in v], axis=0) for v in (das, dbs, hs))
    sums = [dot(da, x, 0, 0), dot(db, x, 0, 0), dot(h, g, 0, 0)]
    for i, (out, value) in enumerate(zip(outs, sums)):
        value = value + olds[i][:, cols] if begun else value
        if not last:
            out[:, cols] = value
        else:
            out[...] = value.astype(HALF).T if i < 2 else value.astype(HALF)


def grads(chunks, olds=(), last=True, tile=512):
    width, hidden = chunks[0][0].shape[1], chunks[0][2].shape[1]
    if last:
        shapes = [(width, hidden), (width, hidden), (hidden, width)]
        out_shape = [jax.ShapeDtypeStruct(s, HALF) for s in shapes]
        out_specs = [pl.BlockSpec((tile, hidden), lambda i: (i, 0))] * 2
        out_specs += [pl.BlockSpec((hidden, tile), lambda i: (0, i))]
    else:
        out_shape, out_specs = [kept((hidden, width), FULL)] * 3, [VMEM] * 3
    return pl.pallas_call(
        functools.partial(grads_kernel, len(chunks), bool(olds), last, tile),
        grid=(width // tile,),
        out_shape=out_shape,
        in_specs=[VMEM] * (5 * len(chunks) + len(olds)),
        out_specs=out_specs,
        name="grads",
        compiler_params=ROOM,
    )(*[c[i] for i in range(5) for c in chunks], *olds)


def combine_kernel(experts, count, mine_ref, other_ref, *refs):
    got, outs = refs[:count], refs[count:]
    home, _ = position(experts)
    cap = got[0].shape[1]
    for side, code_ref in enumerate((mine_ref, other_ref)):
        pick, _ = picks(code_ref[...], home, range(count), cap)
        rows = jnp.concatenate([jnp.where(p, 1.0, 0.0).astype(HALF) for p in pick], axis=0)
        back = jnp.concatenate([r[side] for r in got], axis=0)
        outs[side][...] = dot(rows, back, 0, 0).astype(HALF)


def combine(mine, other, got, experts):
    width, rows = got[0].shape[2], mine.shape[1]
    return pl.pallas_call(
        functools.partial(combine_kernel, experts, len(got)),
        out_shape=[kept((rows, width), HALF)] * 2,
        in_specs=[VMEM] * (2 + len(got)),
        out_specs=[VMEM] * 2,
        name="combine",
        compiler_params=ROOM,
    )(mine, other, *got)


def final_kernel(experts, offsets, code_ref, near_ref, far_ref, *refs):
    got, out = refs[:-1], refs[-1]
    home, _ = position(experts)
    pick, _ = picks(code_ref[...], home, offsets, got[0].shape[0])
    rows = jnp.concatenate([jnp.where(p, 1.0, 0.0).astype(HALF) for p in pick], axis=0)
    back = jnp.concatenate([r[...] for r in got], axis=0)
    total = near_ref[...].astype(FULL) + far_ref[...].astype(FULL) + dot(rows, back, 0, 0)
    out[0] = total.astype(HALF)


def final(code, near, far, offsets, got, experts):
    rows, width = near.shape
    return pl.pallas_call(
        functools.partial(final_kernel, experts, offsets),
        out_shape=jax.ShapeDtypeStruct((1, rows, width), HALF),
        in_specs=[VMEM] * (3 + len(got)),
        out_specs=VMEM,
        name="final",
        compiler_params=ROOM,
    )(code, near, far, *got)


def route_kernel(experts, code_ref, slots_ref, *refs):
    ends, out = refs[:-1], refs[-1]
    home, _ = position(experts)
    code = code_ref[...]
    top, cap = code.shape[0] // 2, slots_ref.shape[1]
    pick, _ = picks(code, home, range(experts), cap)
    values = [slots_ref[o : o + 1] for o in range(slots_ref.shape[0])]
    values += [ends[i][...] + ends[i + 1][...] for i in range(0, len(ends), 2)]
    named = [
        lax.dot_general(
            jnp.broadcast_to(v, (8, cap)),
            jnp.where(p, 1.0, 0.0),
            (((1,), (0,)), ((), ())),
            precision=lax.Precision.HIGHEST,
            preferred_element_type=FULL,
        )[:1]
        for p, v in zip(pick, values)
    ]
    for k in range(top):
        near = code[k : k + 1].astype(jnp.int32) ^ home
        chosen = [jnp.where(near == o, named[o], 0.0) for o in range(experts)]
        total = functools.reduce(jnp.add, chosen) / code[top + k : top + k + 1]
        out[k : k + 1] = total.astype(HALF)


def route(code, slots, ends, experts):
    return pl.pallas_call(
        functools.partial(route_kernel, experts),
        out_shape=jax.ShapeDtypeStruct((code.shape[0] // 2, code.shape[1]), HALF),
        in_specs=[VMEM] * (2 + len(ends)),
        out_specs=VMEM,
        name="route",
        compiler_params=ROOM,
    )(code, slots, *ends)


def body(tokens, routes, probs, cotangent, w_gate, w_up, w_down):
    units = lax.axis_size("expert")
    experts = units // 2
    ring = experts // LINE
    rows, top = routes.shape[1:]
    cap = 2 * rows * top // experts
    wg, wu, wd = load(w_gate[0], w_up[0], w_down[0])

    def along(value, hops):
        step = 2 * ring

        def target(i):
            return hops[i // step] * step + i % step if i // step in hops else None

        return moved(value, target)

    code = jnp.concatenate([routes[0].astype(FULL).T, probs[0].astype(FULL).T], axis=0)
    sides = []
    for own in (tokens[0], cotangent[0]):
        side1 = along(own, {0: 1, 1: 0, 2: 3, 3: 2})
        side2 = along(own, {1: 2, 2: 1})
        side3 = along(side1, {1: 2, 2: 1})
        side4 = along(side2, {1: 0, 2: 3})
        side5 = along(side3, {1: 0, 2: 3})
        sides.append([[own], [side1], [side3, side4], [side2, side5]])
    codes = [code] + [shifted(code, 2 * ring * j) for j in range(1, LINE)]
    mirror = shifted(code, 1, 1)
    lower = shifted(code, 0, 1, 1)

    near, far = {}, {}
    for j in range(LINE):
        picked = select(codes[j], sides[0][j], sides[1][j], experts, cap)
        for d, block in enumerate(picked):
            o = j * ring + d
            near[o] = block if d == 0 else shifted(block, 2 * d)
            far[o] = shifted(near[o], 1)

    groups = groups_of(experts)
    last = list(range(experts - 2, experts))
    chunks, near_rg, far_rg, got = [], {}, {}, {}
    for group in groups:
        near_group, far_group = [near[o] for o in group], [far[o] for o in group]
        reduced = group[0] in last
        chunk, rg, parts = phase(near_group, far_group, wg, wu, wd, reduced)
        chunks.append(chunk)
        for i, o in enumerate(group):
            near_rg[o], far_rg[o] = rg[i], rg[len(group) + i]
            if reduced:
                partner = shifted(parts[1], 1, 1)
                total = (parts[0] + partner.astype(FULL)).astype(HALF)
                got[o] = shifted(total, 2 * o, 1, 1)
            else:
                got[o] = parts[i] if o == 0 else shifted(parts[i], 2 * o, 1)

    begun = grads(chunks[:1], last=False)
    g_gate, g_up, g_down = grads(chunks[1:], begun)

    early = [o for o in range(experts) if o not in last]
    slots = jnp.stack([near_rg[o] for o in early])
    slots += shifted(jnp.stack([far_rg[o] for o in early]), 1)
    for bit in range(experts.bit_length() - 1):
        high = [o for o in early if o >> bit & 1]
        taken = shifted(jnp.stack([slots[o] for o in high]), 2 << bit)
        slots = jnp.stack([taken[high.index(o)] if o in high else slots[o] for o in early])
    ends = [
        shifted(rg[None], 2 * o + side)
        for o in last
        for side, rg in enumerate((near_rg[o], far_rg[o]))
    ]
    route_grad = route(code, slots, ends, experts).T

    dx_near, dx_far = combine(code, mirror, [got[o] for o in early], experts)
    below = shifted(dx_near, 0, 1, 1)
    across = shifted(dx_far, 1, 1, 1)
    upstream = final(lower, below, across, last, [got[o] for o in last], experts)
    return (upstream, route_grad[None], g_gate[None], g_up[None], g_down[None])


def solution(mesh):
    rows, columns = P("section", "expert", None), P("section", None, "expert")
    in_specs = (rows, rows, rows, rows, columns, columns, rows)
    out_specs = (rows, rows, columns, columns, rows)

    return jax.shard_map(body, mesh=mesh, in_specs=in_specs, out_specs=out_specs, check_vma=False)
```

```python
import functools

import jax
import jax.numpy as jnp
from jax import lax
from jax.experimental import pallas as pl
from jax.experimental.pallas import tpu as pltpu
from jax.sharding import PartitionSpec as P


AXES = ("section", "expert")
HALF, FULL = jnp.bfloat16, jnp.float32
LINE = 4
VMEM = pl.BlockSpec(memory_space=pltpu.VMEM)
ANY = pl.BlockSpec(memory_space=pl.ANY)
ROOM = pltpu.CompilerParams(vmem_limit_bytes=28 << 20)


def moved(value, target, first=0, down=0):
    sections, units = lax.axis_size("section"), lax.axis_size("expert")
    pairs = [
        (s * units + i, (s - down) * units + target(i))
        for s in range(first, sections)
        for i in range(units)
        if target(i) is not None
    ]
    return lax.ppermute(value, AXES, pairs)


def shifted(value, mask, first=0, down=0):
    return moved(value, lambda i: i ^ mask, first, down)


def groups_of(experts):
    ring = experts // LINE
    head = [list(range(i, min(i + ring, experts - 2))) for i in range(0, experts - 2, ring)]
    return head + [[experts - 2], [experts - 1]]


def kept(shape, kind):
    return pltpu.VMEM(shape, kind)


def position(experts):
    home = lax.axis_index("expert") // 2
    line = home // (experts // LINE)
    return home, jnp.logical_or(line == 1, line == 2)


def dot(a, b, ca, cb):
    return lax.dot_general(a, b, (((ca,), (cb,)), ((), ())), preferred_element_type=FULL)


def picks(code, home, offsets, cap):
    top, rows = code.shape[0] // 2, code.shape[1]
    near = [code[k : k + 1].astype(jnp.int32) ^ home for k in range(top)]
    hits = [[n == o for n in near] for o in offsets]
    named = jnp.concatenate(
        [functools.reduce(jnp.logical_or, h).astype(FULL) for h in hits], axis=0
    )
    weight = [
        functools.reduce(
            jnp.add, [jnp.where(h[k], code[top + k : top + k + 1], 0.0) for k in range(top)]
        )
        for h in hits
    ]
    earlier = (
        lax.broadcasted_iota(jnp.int32, (rows, rows), 0)
        < lax.broadcasted_iota(jnp.int32, (rows, rows), 1)
    )
    place = dot(named.astype(HALF), earlier.astype(FULL).astype(HALF), 1, 0)
    place = jnp.where(named > 0, place, -1.0)
    slot = lax.broadcasted_iota(jnp.int32, (cap, rows), 0).astype(FULL)
    return [slot == place[i : i + 1] for i in range(len(offsets))], weight


def load_kernel(*refs):
    count, sem = len(refs) // 2, refs[-1]
    copies = [pltpu.make_async_copy(refs[i], refs[count + i], sem.at[i]) for i in range(count)]
    for copy in copies:
        copy.start()
    for copy in copies:
        copy.wait()


def load(*arrays):
    return pl.pallas_call(
        load_kernel,
        out_shape=[kept(v.shape, v.dtype) for v in arrays],
        in_specs=[ANY] * len(arrays),
        out_specs=[VMEM] * len(arrays),
        scratch_shapes=[pltpu.SemaphoreType.DMA((len(arrays),))],
        name="load",
        compiler_params=ROOM,
    )(*arrays)


def select_kernel(sources, experts, cap, code_ref, *refs):
    ring = experts // LINE
    home, inner = position(experts)
    from_x, from_g = refs[:sources], refs[sources : 2 * sources]
    out, (x_held, g_held, sem) = refs[2 * sources : 2 * sources + ring], refs[-3:]

    def fetch(i):
        pltpu.make_async_copy(from_x[i], x_held, sem.at[0]).start()
        pltpu.make_async_copy(from_g[i], g_held, sem.at[1]).start()

    if sources == 1:
        fetch(0)
    else:
        pl.when(inner)(lambda: fetch(0))
        pl.when(jnp.logical_not(inner))(lambda: fetch(1))
    pick, weight = picks(code_ref[...], home, range(ring), cap)
    rows_x = jnp.concatenate([jnp.where(p, 1.0, 0.0) for p in pick], axis=0).astype(HALF)
    rows_g = jnp.concatenate([jnp.where(p, w, 0.0) for p, w in zip(pick, weight)], axis=0)
    pltpu.make_async_copy(from_x[0], x_held, sem.at[0]).wait()
    x = dot(rows_x, x_held[...], 1, 0).astype(HALF)
    for d in range(ring):
        out[d][0] = x[d * cap : (d + 1) * cap]
    pltpu.make_async_copy(from_g[0], g_held, sem.at[1]).wait()
    g = dot(rows_g.astype(HALF), g_held[...], 1, 0).astype(HALF)
    for d in range(ring):
        out[d][1] = g[d * cap : (d + 1) * cap]


def select(code, from_x, from_g, experts, cap):
    rows, width = from_x[0].shape
    ring = experts // LINE
    return pl.pallas_call(
        functools.partial(select_kernel, len(from_x), experts, cap),
        out_shape=[kept((2, cap, width), HALF)] * ring,
        in_specs=[VMEM] + [ANY] * (2 * len(from_x)),
        out_specs=[VMEM] * ring,
        scratch_shapes=[pltpu.VMEM((rows, width), HALF)] * 2 + [pltpu.SemaphoreType.DMA((2,))],
        name="select",
        compiler_params=ROOM,
    )(code, *from_x, *from_g)


def phase_kernel(size, reduced, *refs):
    near, far, (wg, wu, wd) = refs[:size], refs[size : 2 * size], refs[2 * size : 2 * size + 3]
    x_ref, g_ref, da_ref, db_ref, h_ref, rg_ref, *parts, sem = refs[2 * size + 3 :]
    cap = near[0].shape[1]
    for which, held in enumerate((x_ref, g_ref)):
        for i, ref in enumerate(near + far):
            rows = held.at[pl.ds(i * cap, cap)]
            pltpu.make_async_copy(ref.at[which], rows, sem.at[which]).start()
    pltpu.make_async_copy(x_ref, x_ref, sem.at[0]).wait()
    a = dot(x_ref[...], wg[...], 1, 0)
    b = dot(x_ref[...], wu[...], 1, 0)
    pltpu.make_async_copy(g_ref, g_ref, sem.at[1]).wait()
    q = dot(g_ref[...], wd[...], 1, 1)
    sig = jax.nn.sigmoid(a)
    act = a * sig
    h = (act * b).astype(HALF)
    da = (q * b * sig * (1.0 + a * (1.0 - sig))).astype(HALF)
    db = (q * act).astype(HALF)
    h_ref[...], da_ref[...], db_ref[...] = h, da, db
    rg_ref[...] = jnp.sum((q * h.astype(FULL)).reshape(2 * size, cap, -1), axis=2)
    part = dot(da, wg[...], 1, 1) + dot(db, wu[...], 1, 1)
    for i in range(size):
        for side in range(2):
            start = (side * size + i) * cap
            piece = part[start : start + cap]
            if reduced:
                parts[2 * i + side][...] = piece if side == 0 else piece.astype(HALF)
            else:
                parts[i][side] = piece.astype(HALF)


def phase(near, far, wg, wu, wd, reduced):
    size = len(near)
    _, cap, width = near[0].shape
    rows, hidden = 2 * size * cap, wg.shape[1]
    if reduced:
        parts = [kept((cap, width), t) for t in (FULL, HALF)] * size
    else:
        parts = [kept((2, cap, width), HALF)] * size
    out = pl.pallas_call(
        functools.partial(phase_kernel, size, reduced),
        out_shape=[kept((rows, width), HALF)] * 2
        + [kept((rows, hidden), HALF)] * 3
        + [kept((2 * size, cap), FULL)]
        + parts,
        in_specs=[ANY] * (2 * size) + [VMEM] * 3,
        out_specs=[VMEM] * (6 + len(parts)),
        scratch_shapes=[pltpu.SemaphoreType.DMA((2,))],
        name="phase",
        compiler_params=ROOM,
    )(*near, *far, wg, wu, wd)
    return out[:5], out[5], out[6:]


def grads_kernel(count, begun, last, tile, *refs):
    xs, gs, das, dbs, hs = (refs[i * count : (i + 1) * count] for i in range(5))
    olds, outs = refs[5 * count : -3], refs[-3:]
    start = pl.multiple_of(pl.program_id(0) * tile, tile)
    cols = pl.ds(start, tile)
    x = jnp.concatenate([r[:, cols] for r in xs], axis=0)
    g = jnp.concatenate([r[:, cols] for r in gs], axis=0)
    da, db, h = (jnp.concatenate([r[...] for r in v], axis=0) for v in (das, dbs, hs))
    sums = [dot(da, x, 0, 0), dot(db, x, 0, 0), dot(h, g, 0, 0)]
    for i, (out, value) in enumerate(zip(outs, sums)):
        value = value + olds[i][:, cols] if begun else value
        if not last:
            out[:, cols] = value
        else:
            out[...] = value.astype(HALF).T if i < 2 else value.astype(HALF)


def grads(chunks, olds=(), last=True, tile=512):
    width, hidden = chunks[0][0].shape[1], chunks[0][2].shape[1]
    if last:
        shapes = [(width, hidden), (width, hidden), (hidden, width)]
        out_shape = [jax.ShapeDtypeStruct(s, HALF) for s in shapes]
        out_specs = [pl.BlockSpec((tile, hidden), lambda i: (i, 0))] * 2
        out_specs += [pl.BlockSpec((hidden, tile), lambda i: (0, i))]
    else:
        out_shape, out_specs = [kept((hidden, width), FULL)] * 3, [VMEM] * 3
    return pl.pallas_call(
        functools.partial(grads_kernel, len(chunks), bool(olds), last, tile),
        grid=(width // tile,),
        out_shape=out_shape,
        in_specs=[VMEM] * (5 * len(chunks) + len(olds)),
        out_specs=out_specs,
        name="grads",
        compiler_params=ROOM,
    )(*[c[i] for i in range(5) for c in chunks], *olds)


def combine_kernel(experts, count, mine_ref, other_ref, *refs):
    got, outs = refs[:count], refs[count:]
    home, _ = position(experts)
    cap = got[0].shape[1]
    for side, code_ref in enumerate((mine_ref, other_ref)):
        pick, _ = picks(code_ref[...], home, range(count), cap)
        rows = jnp.concatenate([jnp.where(p, 1.0, 0.0).astype(HALF) for p in pick], axis=0)
        back = jnp.concatenate([r[side] for r in got], axis=0)
        outs[side][...] = dot(rows, back, 0, 0).astype(HALF)


def combine(mine, other, got, experts):
    width, rows = got[0].shape[2], mine.shape[1]
    return pl.pallas_call(
        functools.partial(combine_kernel, experts, len(got)),
        out_shape=[kept((rows, width), HALF)] * 2,
        in_specs=[VMEM] * (2 + len(got)),
        out_specs=[VMEM] * 2,
        name="combine",
        compiler_params=ROOM,
    )(mine, other, *got)


def final_kernel(experts, offsets, code_ref, near_ref, far_ref, *refs):
    got, out = refs[:-1], refs[-1]
    home, _ = position(experts)
    pick, _ = picks(code_ref[...], home, offsets, got[0].shape[0])
    rows = jnp.concatenate([jnp.where(p, 1.0, 0.0).astype(HALF) for p in pick], axis=0)
    back = jnp.concatenate([r[...] for r in got], axis=0)
    total = near_ref[...].astype(FULL) + far_ref[...].astype(FULL) + dot(rows, back, 0, 0)
    out[0] = total.astype(HALF)


def final(code, near, far, offsets, got, experts):
    rows, width = near.shape
    return pl.pallas_call(
        functools.partial(final_kernel, experts, offsets),
        out_shape=jax.ShapeDtypeStruct((1, rows, width), HALF),
        in_specs=[VMEM] * (3 + len(got)),
        out_specs=VMEM,
        name="final",
        compiler_params=ROOM,
    )(code, near, far, *got)


def route_kernel(experts, code_ref, slots_ref, *refs):
    ends, out = refs[:-1], refs[-1]
    home, _ = position(experts)
    code = code_ref[...]
    top, cap = code.shape[0] // 2, slots_ref.shape[1]
    pick, _ = picks(code, home, range(experts), cap)
    values = [slots_ref[o : o + 1] for o in range(slots_ref.shape[0])]
    values += [ends[i][...] + ends[i + 1][...] for i in range(0, len(ends), 2)]
    named = [
        lax.dot_general(
            jnp.broadcast_to(v, (8, cap)),
            jnp.where(p, 1.0, 0.0),
            (((1,), (0,)), ((), ())),
            precision=lax.Precision.HIGHEST,
            preferred_element_type=FULL,
        )[:1]
        for p, v in zip(pick, values)
    ]
    for k in range(top):
        near = code[k : k + 1].astype(jnp.int32) ^ home
        chosen = [jnp.where(near == o, named[o], 0.0) for o in range(experts)]
        total = functools.reduce(jnp.add, chosen) / code[top + k : top + k + 1]
        out[k : k + 1] = total.astype(HALF)


def route(code, slots, ends, experts):
    return pl.pallas_call(
        functools.partial(route_kernel, experts),
        out_shape=jax.ShapeDtypeStruct((code.shape[0] // 2, code.shape[1]), HALF),
        in_specs=[VMEM] * (2 + len(ends)),
        out_specs=VMEM,
        name="route",
        compiler_params=ROOM,
    )(code, slots, *ends)


def body(tokens, routes, probs, cotangent, w_gate, w_up, w_down):
    units = lax.axis_size("expert")
    experts = units // 2
    ring = experts // LINE
    rows, top = routes.shape[1:]
    cap = 2 * rows * top // experts
    wg, wu, wd = load(w_gate[0], w_up[0], w_down[0])

    def along(value, hops):
        step = 2 * ring

        def target(i):
            return hops[i // step] * step + i % step if i // step in hops else None

        return moved(value, target)

    code = jnp.concatenate([routes[0].astype(FULL).T, probs[0].astype(FULL).T], axis=0)
    sides = []
    for own in (tokens[0], cotangent[0]):
        side1 = along(own, {0: 1, 1: 0, 2: 3, 3: 2})
        side2 = along(own, {1: 2, 2: 1})
        side3 = along(side1, {1: 2, 2: 1})
        side4 = along(side2, {1: 0, 2: 3})
        side5 = along(side3, {1: 0, 2: 3})
        sides.append([[own], [side1], [side3, side4], [side2, side5]])
    codes = [code] + [shifted(code, 2 * ring * j) for j in range(1, LINE)]
    mirror = shifted(code, 1, 1)
    lower = shifted(code, 0, 1, 1)

    near, far = {}, {}
    for j in range(LINE):
        picked = select(codes[j], sides[0][j], sides[1][j], experts, cap)
        for d, block in enumerate(picked):
            o = j * ring + d
            near[o] = block if d == 0 else shifted(block, 2 * d)
            far[o] = shifted(near[o], 1)

    groups = groups_of(experts)
    last = list(range(experts - 2, experts))
    chunks, near_rg, far_rg, got = [], {}, {}, {}
    for group in groups:
        near_group, far_group = [near[o] for o in group], [far[o] for o in group]
        reduced = group[0] in last
        chunk, rg, parts = phase(near_group, far_group, wg, wu, wd, reduced)
        chunks.append(chunk)
        for i, o in enumerate(group):
            near_rg[o], far_rg[o] = rg[i], rg[len(group) + i]
            if reduced:
                partner = shifted(parts[1], 1, 1)
                total = (parts[0] + partner.astype(FULL)).astype(HALF)
                got[o] = shifted(total, 2 * o, 1, 1)
            else:
                got[o] = parts[i] if o == 0 else shifted(parts[i], 2 * o, 1)

    begun = grads(chunks[:2], last=False)
    g_gate, g_up, g_down = grads(chunks[2:], begun)

    early = [o for o in range(experts) if o not in last]
    slots = jnp.stack([near_rg[o] for o in early])
    slots += shifted(jnp.stack([far_rg[o] for o in early]), 1)
    for bit in range(experts.bit_length() - 1):
        high = [o for o in early if o >> bit & 1]
        taken = shifted(jnp.stack([slots[o] for o in high]), 2 << bit)
        slots = jnp.stack([taken[high.index(o)] if o in high else slots[o] for o in early])
    ends = [
        shifted(rg[None], 2 * o + side)
        for o in last
        for side, rg in enumerate((near_rg[o], far_rg[o]))
    ]
    route_grad = route(code, slots, ends, experts).T

    dx_near, dx_far = combine(code, mirror, [got[o] for o in early], experts)
    below = shifted(dx_near, 0, 1, 1)
    across = shifted(dx_far, 1, 1, 1)
    upstream = final(lower, below, across, last, [got[o] for o in last], experts)
    return (upstream, route_grad[None], g_gate[None], g_up[None], g_down[None])


def solution(mesh):
    rows, columns = P("section", "expert", None), P("section", None, "expert")
    in_specs = (rows, rows, rows, rows, columns, columns, rows)
    out_specs = (rows, rows, columns, columns, rows)

    return jax.shard_map(body, mesh=mesh, in_specs=in_specs, out_specs=out_specs, check_vma=False)
```

```python
import functools

import jax
import jax.numpy as jnp
from jax import lax
from jax.experimental import pallas as pl
from jax.experimental.pallas import tpu as pltpu
from jax.sharding import PartitionSpec as P


AXES = ("section", "expert")
HALF, FULL = jnp.bfloat16, jnp.float32
LINE = 4
VMEM = pl.BlockSpec(memory_space=pltpu.VMEM)
ANY = pl.BlockSpec(memory_space=pl.ANY)
HBM = pl.BlockSpec(memory_space=pltpu.HBM)
ROOM = pltpu.CompilerParams(vmem_limit_bytes=28 << 20)


def moved(value, target, first=0, down=0):
    sections, units = lax.axis_size("section"), lax.axis_size("expert")
    pairs = [
        (s * units + i, (s - down) * units + target(i))
        for s in range(first, sections)
        for i in range(units)
        if target(i) is not None
    ]
    return lax.ppermute(value, AXES, pairs)


def shifted(value, mask, first=0, down=0):
    return moved(value, lambda i: i ^ mask, first, down)


def groups_of(experts):
    ring = experts // LINE
    head = [list(range(i, min(i + ring, experts - 2))) for i in range(0, experts - 2, ring)]
    return head + [[experts - 2], [experts - 1]]


def outside(*arrays):
    return [pltpu.with_memory_space_constraint(v, pltpu.HBM) for v in arrays]


def kept(shape, kind):
    return pltpu.VMEM(shape, kind)


def position(experts):
    home = lax.axis_index("expert") // 2
    line = home // (experts // LINE)
    return home, jnp.logical_or(line == 1, line == 2)


def dot(a, b, ca, cb):
    return lax.dot_general(a, b, (((ca,), (cb,)), ((), ())), preferred_element_type=FULL)


def picks(code, home, offsets, cap):
    top, rows = code.shape[0] // 2, code.shape[1]
    near = [code[k : k + 1].astype(jnp.int32) ^ home for k in range(top)]
    hits = [[n == o for n in near] for o in offsets]
    named = jnp.concatenate(
        [functools.reduce(jnp.logical_or, h).astype(FULL) for h in hits], axis=0
    )
    weight = [
        functools.reduce(
            jnp.add, [jnp.where(h[k], code[top + k : top + k + 1], 0.0) for k in range(top)]
        )
        for h in hits
    ]
    earlier = (
        lax.broadcasted_iota(jnp.int32, (rows, rows), 0)
        < lax.broadcasted_iota(jnp.int32, (rows, rows), 1)
    )
    place = dot(named.astype(HALF), earlier.astype(FULL).astype(HALF), 1, 0)
    place = jnp.where(named > 0, place, -1.0)
    slot = lax.broadcasted_iota(jnp.int32, (cap, rows), 0).astype(FULL)
    return [slot == place[i : i + 1] for i in range(len(offsets))], weight


def load_kernel(*refs):
    count, sem = len(refs) // 2, refs[-1]
    copies = [pltpu.make_async_copy(refs[i], refs[count + i], sem.at[i]) for i in range(count)]
    for copy in copies:
        copy.start()
    for copy in copies:
        copy.wait()


def load(*arrays):
    return pl.pallas_call(
        load_kernel,
        out_shape=[kept(v.shape, v.dtype) for v in arrays],
        in_specs=[HBM] * len(arrays),
        out_specs=[VMEM] * len(arrays),
        scratch_shapes=[pltpu.SemaphoreType.DMA((len(arrays),))],
        name="load",
        compiler_params=ROOM,
    )(*outside(*arrays))


def choose(x_ref, g_ref, code, home, ring, cap, out):
    rows = code.shape[1]
    pick, weight = picks(code, home, range(ring), cap)
    rows_x = jnp.concatenate([jnp.where(p, 1.0, 0.0) for p in pick], axis=0).astype(HALF)
    rows_g = jnp.concatenate([jnp.where(p, w, 0.0) for p, w in zip(pick, weight)], axis=0)
    x = dot(rows_x, x_ref[:rows], 1, 0).astype(HALF)
    g = dot(rows_g.astype(HALF), g_ref[...], 1, 0).astype(HALF)
    for d in range(ring):
        out[d][0] = x[d * cap : (d + 1) * cap]
        out[d][1] = g[d * cap : (d + 1) * cap]


def start_kernel(experts, cap, routes_ref, probs_ref, x_ref, g_ref, *refs):
    own, code_ref, out, (routes, probs, g_held, sem) = refs[0], refs[1], refs[2:-4], refs[-4:]
    (top, rows), width = routes_ref.shape, x_ref.shape[1]
    copies = [
        pltpu.make_async_copy(routes_ref, routes, sem.at[0]),
        pltpu.make_async_copy(probs_ref, probs, sem.at[1]),
        pltpu.make_async_copy(x_ref, own.at[pl.ds(0, rows)], sem.at[2]),
        pltpu.make_async_copy(g_ref, g_held, sem.at[3]),
    ]
    for copy in copies:
        copy.start()
    home, _ = position(experts)
    copies[0].wait()
    copies[1].wait()
    code = jnp.concatenate([routes[...].astype(FULL), probs[...].astype(FULL)], axis=0)
    code_ref[...] = code
    spare = own.shape[0] - rows
    lead = jnp.concatenate([code, jnp.zeros((spare - 2 * top, rows), FULL)], axis=0)
    own[rows:, :rows] = lead.astype(HALF)
    own[rows:, rows:] = jnp.zeros((spare, width - rows), HALF)
    copies[2].wait()
    copies[3].wait()
    choose(own, g_held, code, home, experts // LINE, cap, out)


def start(routes, probs, x, g, experts, cap):
    (top, rows), width = routes.shape, x.shape[1]
    ring = experts // LINE
    out = pl.pallas_call(
        functools.partial(start_kernel, experts, cap),
        out_shape=[kept((rows + 16, width), HALF), kept((2 * top, rows), FULL)]
        + [kept((2, cap, width), HALF)] * ring,
        in_specs=[HBM] * 4,
        out_specs=[VMEM] * (2 + ring),
        scratch_shapes=[
            pltpu.VMEM(routes.shape, routes.dtype),
            pltpu.VMEM(probs.shape, probs.dtype),
            pltpu.VMEM((rows, width), HALF),
            pltpu.SemaphoreType.DMA((4,)),
        ],
        name="start",
        compiler_params=ROOM,
    )(*outside(routes, probs, x, g))
    return out[0], out[1], out[2:]


def select_kernel(sources, experts, cap, top, *refs):
    from_x, from_g, out = refs[:sources], refs[sources : 2 * sources], refs[2 * sources : -3]
    x_held, g_held, sem = refs[-3:]
    home, inner = position(experts)
    rows = g_held.shape[0]

    def fetch(i):
        pltpu.make_async_copy(from_x[i], x_held, sem.at[0]).start()
        pltpu.make_async_copy(from_g[i], g_held, sem.at[1]).start()

    if sources == 1:
        fetch(0)
    else:
        pl.when(inner)(lambda: fetch(0))
        pl.when(jnp.logical_not(inner))(lambda: fetch(1))
    pltpu.make_async_copy(from_x[0], x_held, sem.at[0]).wait()
    pltpu.make_async_copy(from_g[0], g_held, sem.at[1]).wait()
    code = x_held[rows:, :rows].astype(FULL)[: 2 * top]
    choose(x_held, g_held, code, home, experts // LINE, cap, out)


def select(from_x, from_g, experts, cap, top):
    rows, width = from_g[0].shape
    ring = experts // LINE
    return pl.pallas_call(
        functools.partial(select_kernel, len(from_x), experts, cap, top),
        out_shape=[kept((2, cap, width), HALF)] * ring,
        in_specs=[ANY] * (2 * len(from_x)),
        out_specs=[VMEM] * ring,
        scratch_shapes=[
            pltpu.VMEM(from_x[0].shape, HALF),
            pltpu.VMEM((rows, width), HALF),
            pltpu.SemaphoreType.DMA((2,)),
        ],
        name="select",
        compiler_params=ROOM,
    )(*from_x, *from_g)


def merge_kernel(plan, *refs):
    ins, outs = refs[: -len(plan)], refs[-len(plan) :]
    for out, rows in zip(outs, plan):
        for i, terms in enumerate(rows):
            parts = [ins[k][r : r + 1] for k, r in terms]
            out[i : i + 1] = functools.reduce(jnp.add, parts)


def merge(plan, *arrays):
    return pl.pallas_call(
        functools.partial(merge_kernel, plan),
        out_shape=[kept((len(rows), arrays[0].shape[1]), FULL) for rows in plan],
        in_specs=[VMEM] * len(arrays),
        out_specs=[VMEM] * len(plan),
        name="merge",
        compiler_params=ROOM,
    )(*arrays)


def phase_kernel(size, reduced, *refs):
    near, far, (wg, wu, wd) = refs[:size], refs[size : 2 * size], refs[2 * size : 2 * size + 3]
    x_ref, g_ref, da_ref, db_ref, h_ref, rg_near, rg_far, *parts, sem = refs[2 * size + 3 :]
    cap = near[0].shape[1]
    for which, held in enumerate((x_ref, g_ref)):
        for i, ref in enumerate(near + far):
            rows = held.at[pl.ds(i * cap, cap)]
            pltpu.make_async_copy(ref.at[which], rows, sem.at[which]).start()
    pltpu.make_async_copy(x_ref, x_ref, sem.at[0]).wait()
    a = dot(x_ref[...], wg[...], 1, 0)
    b = dot(x_ref[...], wu[...], 1, 0)
    pltpu.make_async_copy(g_ref, g_ref, sem.at[1]).wait()
    q = dot(g_ref[...], wd[...], 1, 1)
    sig = jax.nn.sigmoid(a)
    act = a * sig
    h = (act * b).astype(HALF)
    da = (q * b * sig * (1.0 + a * (1.0 - sig))).astype(HALF)
    db = (q * act).astype(HALF)
    h_ref[...], da_ref[...], db_ref[...] = h, da, db
    rg = jnp.sum((q * h.astype(FULL)).reshape(2 * size, cap, -1), axis=2)
    rg_near[...], rg_far[...] = rg[:size], rg[size:]
    part = dot(da, wg[...], 1, 1) + dot(db, wu[...], 1, 1)
    for i in range(size):
        for side in range(2):
            start = (side * size + i) * cap
            piece = part[start : start + cap]
            if reduced:
                parts[2 * i + side][...] = piece if side == 0 else piece.astype(HALF)
            else:
                parts[i][side] = piece.astype(HALF)


def phase(near, far, wg, wu, wd, reduced):
    size = len(near)
    _, cap, width = near[0].shape
    rows, hidden = 2 * size * cap, wg.shape[1]
    if reduced:
        parts = [kept((cap, width), t) for t in (FULL, HALF)] * size
    else:
        parts = [kept((2, cap, width), HALF)] * size
    out = pl.pallas_call(
        functools.partial(phase_kernel, size, reduced),
        out_shape=[kept((rows, width), HALF)] * 2
        + [kept((rows, hidden), HALF)] * 3
        + [kept((size, cap), FULL)] * 2
        + parts,
        in_specs=[ANY] * (2 * size) + [VMEM] * 3,
        out_specs=[VMEM] * (7 + len(parts)),
        scratch_shapes=[pltpu.SemaphoreType.DMA((2,))],
        name="phase",
        compiler_params=ROOM,
    )(*near, *far, wg, wu, wd)
    return out[:5], out[5:7], out[7:]


def grads_kernel(count, begun, last, tile, *refs):
    xs, gs, das, dbs, hs = (refs[i * count : (i + 1) * count] for i in range(5))
    olds, outs = refs[5 * count : -3], refs[-3:]
    start = pl.multiple_of(pl.program_id(0) * tile, tile)
    cols = pl.ds(start, tile)
    x = jnp.concatenate([r[:, cols] for r in xs], axis=0)
    g = jnp.concatenate([r[:, cols] for r in gs], axis=0)
    da, db, h = (jnp.concatenate([r[...] for r in v], axis=0) for v in (das, dbs, hs))
    sums = [dot(da, x, 0, 0), dot(db, x, 0, 0), dot(h, g, 0, 0)]
    for i, (out, value) in enumerate(zip(outs, sums)):
        value = value + olds[i][:, cols] if begun else value
        if not last:
            out[:, cols] = value
        else:
            out[...] = value.astype(HALF).T if i < 2 else value.astype(HALF)


def grads(chunks, olds=(), last=True, tile=512):
    width, hidden = chunks[0][0].shape[1], chunks[0][2].shape[1]
    if last:
        shapes = [(width, hidden), (width, hidden), (hidden, width)]
        out_shape = [jax.ShapeDtypeStruct(s, HALF) for s in shapes]
        out_specs = [pl.BlockSpec((tile, hidden), lambda i: (i, 0))] * 2
        out_specs += [pl.BlockSpec((hidden, tile), lambda i: (0, i))]
    else:
        out_shape, out_specs = [kept((hidden, width), FULL)] * 3, [VMEM] * 3
    return pl.pallas_call(
        functools.partial(grads_kernel, len(chunks), bool(olds), last, tile),
        grid=(width // tile,),
        out_shape=out_shape,
        in_specs=[VMEM] * (5 * len(chunks) + len(olds)),
        out_specs=out_specs,
        input_output_aliases={} if last else {5 * len(chunks) + i: i for i in range(len(olds))},
        name="grads",
        compiler_params=ROOM,
    )(*[c[i] for i in range(5) for c in chunks], *olds)


def combine_kernel(experts, count, mine_ref, other_ref, *refs):
    got, outs = refs[:count], refs[count:]
    home, _ = position(experts)
    cap = got[0].shape[1]
    for side, code_ref in enumerate((mine_ref, other_ref)):
        pick, _ = picks(code_ref[...], home, range(count), cap)
        rows = jnp.concatenate([jnp.where(p, 1.0, 0.0).astype(HALF) for p in pick], axis=0)
        back = jnp.concatenate([r[side] for r in got], axis=0)
        outs[side][...] = dot(rows, back, 0, 0).astype(HALF)


def combine(mine, other, got, experts):
    width, rows = got[0].shape[2], mine.shape[1]
    return pl.pallas_call(
        functools.partial(combine_kernel, experts, len(got)),
        out_shape=[kept((rows, width), HALF)] * 2,
        in_specs=[VMEM] * (2 + len(got)),
        out_specs=[VMEM] * 2,
        name="combine",
        compiler_params=ROOM,
    )(mine, other, *got)


def final_kernel(experts, offsets, code_ref, near_ref, far_ref, *refs):
    got, out = refs[:-1], refs[-1]
    home, _ = position(experts)
    pick, _ = picks(code_ref[...], home, offsets, got[0].shape[0])
    rows = jnp.concatenate([jnp.where(p, 1.0, 0.0).astype(HALF) for p in pick], axis=0)
    back = jnp.concatenate([r[...] for r in got], axis=0)
    total = near_ref[...].astype(FULL) + far_ref[...].astype(FULL) + dot(rows, back, 0, 0)
    out[0] = total.astype(HALF)


def final(code, near, far, offsets, got, experts):
    rows, width = near.shape
    return pl.pallas_call(
        functools.partial(final_kernel, experts, offsets),
        out_shape=jax.ShapeDtypeStruct((1, rows, width), HALF),
        in_specs=[VMEM] * (3 + len(got)),
        out_specs=VMEM,
        name="final",
        compiler_params=ROOM,
    )(code, near, far, *got)


def route_kernel(experts, code_ref, slots_ref, out):
    home, _ = position(experts)
    code = code_ref[...]
    top, cap = code.shape[0] // 2, slots_ref.shape[1]
    pick, _ = picks(code, home, range(experts), cap)
    named = [
        lax.dot_general(
            jnp.broadcast_to(slots_ref[o : o + 1], (8, cap)),
            jnp.where(p, 1.0, 0.0),
            (((1,), (0,)), ((), ())),
            precision=lax.Precision.HIGHEST,
            preferred_element_type=FULL,
        )[:1]
        for o, p in enumerate(pick)
    ]
    for k in range(top):
        near = code[k : k + 1].astype(jnp.int32) ^ home
        chosen = [jnp.where(near == o, named[o], 0.0) for o in range(experts)]
        total = functools.reduce(jnp.add, chosen) / code[top + k : top + k + 1]
        out[k : k + 1] = total.astype(HALF)


def route(code, slots, experts):
    return pl.pallas_call(
        functools.partial(route_kernel, experts),
        out_shape=jax.ShapeDtypeStruct((code.shape[0] // 2, code.shape[1]), HALF),
        in_specs=[VMEM] * 2,
        out_specs=VMEM,
        name="route",
        compiler_params=ROOM,
    )(code, slots)


def body(tokens, routes, probs, cotangent, w_gate, w_up, w_down):
    units = lax.axis_size("expert")
    experts = units // 2
    ring = experts // LINE
    rows, top = routes.shape[1:]
    cap = 2 * rows * top // experts
    wg, wu, wd = load(w_gate[0], w_up[0], w_down[0])

    def along(value, hops):
        step = 2 * ring

        def target(i):
            return hops[i // step] * step + i % step if i // step in hops else None

        return moved(value, target)

    own, code, first = start(
        routes[0].T, probs[0].T, tokens[0], cotangent[0], experts, cap
    )
    sides = []
    for mine in (own, cotangent[0]):
        side1 = along(mine, {0: 1, 1: 0, 2: 3, 3: 2})
        side2 = along(mine, {1: 2, 2: 1})
        side3 = along(side1, {1: 2, 2: 1})
        side4 = along(side2, {1: 0, 2: 3})
        side5 = along(side3, {1: 0, 2: 3})
        sides.append([[mine], [side1], [side3, side4], [side2, side5]])
    mirror = shifted(code, 1, 1)
    lower = shifted(code, 0, 1, 1)

    near, far = {}, {}
    for j in range(LINE):
        picked = select(sides[0][j], sides[1][j], experts, cap, top) if j else first
        for d, block in enumerate(picked):
            o = j * ring + d
            near[o] = block if d == 0 else shifted(block, 2 * d)
            far[o] = shifted(near[o], 1)

    groups = groups_of(experts)
    last = list(range(experts - 2, experts))
    chunks, rgs, near_rg, far_rg, got = [], [], {}, {}, {}
    for number, group in enumerate(groups):
        near_group, far_group = [near[o] for o in group], [far[o] for o in group]
        reduced = group[0] in last
        chunk, rg, parts = phase(near_group, far_group, wg, wu, wd, reduced)
        chunks.append(chunk)
        rgs += rg
        for i, o in enumerate(group):
            near_rg[o], far_rg[o] = (2 * number, i), (2 * number + 1, i)
            if reduced:
                partner = shifted(parts[1], 1, 1)
                total = (parts[0] + partner.astype(FULL)).astype(HALF)
                got[o] = shifted(total, 2 * o, 1, 1)
            else:
                got[o] = parts[i] if o == 0 else shifted(parts[i], 2 * o, 1)

    begun = grads(chunks[:2], last=False)
    begun = grads(chunks[2:-1], begun, last=False)
    g_gate, g_up, g_down = grads(chunks[-1:], begun, tile=1024)

    every = range(experts)
    plan = [[[part[o]] for o in every] for part in (near_rg, far_rg)]
    slots, sent = merge(plan, *rgs)
    rows_in = [[(0, o), (1, o)] for o in every]
    for bit in range(experts.bit_length()):
        taken = shifted(sent, 1 << bit)
        high = [o for o in every if o >> bit & 1]
        more = bit + 1 < experts.bit_length()
        slots, *sent = merge(
            [rows_in] + ([[rows_in[o] for o in high]] if more else []), slots, taken
        )
        sent = sent[0] if more else None
        rows_in = [[(1, high.index(o))] if o in high else [(0, o)] for o in every]
    route_grad = route(code, slots, experts).T

    dx_near, dx_far = combine(code, mirror, [got[o] for o in range(experts - 2)], experts)
    below = shifted(dx_near, 0, 1, 1)
    across = shifted(dx_far, 1, 1, 1)
    upstream = final(lower, below, across, last, [got[o] for o in last], experts)
    return (upstream, route_grad[None], g_gate[None], g_up[None], g_down[None])


def solution(mesh):
    rows, columns = P("section", "expert", None), P("section", None, "expert")
    in_specs = (rows, rows, rows, rows, columns, columns, rows)
    out_specs = (rows, rows, columns, columns, rows)

    return jax.shard_map(body, mesh=mesh, in_specs=in_specs, out_specs=out_specs, check_vma=False)
```
